512 devices in a mesh: dp: 16 (over y, x), expert: 32 (over z, core).
Axes of the slice: x: 4, y: 4, z: 16, core: 2. Of those that a mesh axis runs over, the one named last changes fastest.
Arguments:
- tokens: bfloat16 [65536, 1024], P(('dp', 'expert')), may hold values from -6 to 6
- cotangent: bfloat16 [65536, 1024], P(('dp', 'expert')), may hold values from -4 to 4
- expert_ids: int32 [65536, 8], P(('dp', 'expert')), may hold values from 0 to 31, all different within a row; in each aligned block of 128 rows (0 to 127, 128 to 255, ...) at most 36 rows name the same one
- gate_probs: bfloat16 [65536, 8], P(('dp', 'expert')), may hold values from 0.049804688 to 0.29882812
- w_gate: bfloat16 [32, 1024, 384], P('expert'), may hold values from -0.1875 to 0.1875
- w_up: bfloat16 [32, 1024, 384], P('expert'), may hold values from -0.1875 to 0.1875
- w_down: bfloat16 [32, 384, 1024], P('expert'), may hold values from -0.3125 to 0.3125
Outputs:
- grad_tokens: bfloat16 [65536, 1024], P(('dp', 'expert'))
- grad_probs: bfloat16 [65536, 8], P(('dp', 'expert'))
- grad_w_gate: bfloat16 [32, 1024, 384], P('expert', 'dp')
- grad_w_up: bfloat16 [32, 1024, 384], P('expert', 'dp')
- grad_w_down: bfloat16 [32, 384, 1024], P('expert', 'dp')
The draws below stay inside these ranges and needn't reach their ends.
Inputs may be any that keep to these rules, and one draw needn't show every extreme that they name: `expert_ids`: each row names 8 different experts. Among the rows of one device no expert is named more than 36 times, and in some device's rows some expert is named exactly 36 times.
All inputs are finite; a program needn't handle non-finite values.
Results may differ from the reference program's by a relative error of at most 0.014.
Values may be sent and summed in bfloat16 or wider, within the bound.
A program may use at most 64 MiB of HBM per device.

```python
import math
import jax
import jax.numpy as jnp
import numpy as np
from jax import lax

D = 1024
FF = 384
TOPK = 8
TOK_DEV = 128
EXPERTS = 32
MOST = 36
TOKENS = 65536
N_DP = 16
N_EXPERT = 32


def block_scale(key, extent, pieces, least, top_value):
    gain, own = 1.0, jax.random.fold_in(key, 6)
    for dim, shards_of in pieces:
        draws = jnp.exp(jax.random.uniform(jax.random.fold_in(own, dim), (shards_of,), jnp.float32, least / len(pieces), top_value / len(pieces)))
        gain = gain * jnp.repeat(draws, extent[dim] // shards_of).reshape([-1 if axis == dim else 1 for axis in range(len(extent))])
    return gain


def deal_out(own_key, own, number, rows, number_of, top, limit, lean):
    ranking = jax.random.permutation(own_key, number_of)
    crowded, common = load_shares(number_of, rows * top, limit, lean, True), load_shares(number_of, rows * top, limit, lean, False)
    places = jnp.arange(number_of)

    def named(lengths, offset_by):
        used = int((lengths > 0).sum())
        fixed = max(1, used // 4)
        moved = fixed + (places - fixed + offset_by * (used - fixed)) % max(1, number_of - fixed)
        return jnp.zeros((number_of,), jnp.int32).at[ranking[jnp.where(places < fixed, places, moved)]].set(jnp.asarray(lengths, jnp.int32))

    lengths = jnp.where(number % 4 == 0, named(crowded, number // 4), named(common, number - number // 4 - 1))
    mixed = jax.random.permutation(jax.random.fold_in(own, 3), number_of)
    donor, taker = mixed[0:number_of // 2 * 2:2], mixed[1:number_of // 2 * 2:2]
    margin = jnp.minimum(lengths[donor] - 1, limit - lengths[taker]) // 2
    margin = jnp.where((donor == ranking[0]) | (taker == ranking[0]) | (lengths[taker] == 0), 0, jnp.maximum(margin, 0))
    moved = jax.random.randint(jax.random.fold_in(own, 4), (number_of // 2,), 0, 1 << 20) % (margin + 1)
    lengths = lengths.at[donor].add(-moved).at[taker].add(moved)
    labels = jnp.searchsorted(jnp.cumsum(lengths), jnp.arange(rows * top), side="right").astype(jnp.int32)
    table = labels.reshape(top, rows).T
    table = table[jax.random.permutation(jax.random.fold_in(own, 1), rows)]
    offset_by = jax.random.randint(jax.random.fold_in(own, 2), (rows, 1), 0, top)
    return jnp.take_along_axis(table, (jnp.arange(top)[None, :] + offset_by) % top, axis=1)


def load_shares(amount, total, limit, lean, full):
    loads = [(1 << 20) // math.isqrt(rank ** lean) + 1 for rank in range(1, amount + 1)]
    largest = limit if full else min(limit, max(-(-total // amount), total * loads[0] // sum(loads)))
    least = 1 if total - largest >= amount - 1 else 0
    holding, spare = [largest] + [least] * (amount - 1), total - largest - least * (amount - 1)
    while spare > 0:
        free = [i for i in range(1, amount) if holding[i] < largest] or [i for i in range(1, amount) if holding[i] < limit]
        whole, budget = sum([loads[i] for i in free]), spare
        for i in free:
            addition = min(limit - holding[i], max(1, budget * loads[i] // whole), spare)
            holding[i] = holding[i] + addition
            spare = spare - addition
    return np.array(holding)


def centred(stream_key, extent, scale, most, split=(), kind=jnp.bfloat16):
    factor_of = block_scale(stream_key, extent, split, -0.22, 0.18) if split else 1.0
    drawn = jax.random.normal(stream_key, extent, jnp.float32) * scale * factor_of
    return jnp.minimum(jnp.maximum(drawn, -most), most).astype(kind)


def setup_inputs(seed: int = 0) -> dict:
    key_list = jax.random.split(jax.random.key(seed), 8)
    tokens = centred(key_list[0], (TOKENS, D), 1.0, 6.0, ((0, 512),))
    cotangent = centred(key_list[1], (TOKENS, D), 0.25, 4.0, ((0, 512),))
    expert_ids_keys = jax.random.split(jax.random.fold_in(key_list[2], 1), TOKENS // TOK_DEV)
    expert_ids_turns = jax.random.permutation(jax.random.fold_in(key_list[2], 3), TOKENS // TOK_DEV)
    expert_ids = jax.vmap(lambda own, number: deal_out(jax.random.fold_in(key_list[2], 2), own, number, TOK_DEV, EXPERTS, TOPK, MOST, 1))(expert_ids_keys, expert_ids_turns).reshape((TOKENS, TOPK))
    gate_probs = jnp.clip(0.049804688 + 0.24902344 * jax.random.uniform(key_list[3], (TOKENS, TOPK), jnp.float32) ** block_scale(key_list[3], (TOKENS, TOPK), ((0, 512),), -0.2, 0.2), 0.049804688, 0.29882812).astype(jnp.bfloat16)
    w_gate = centred(key_list[4], (EXPERTS, D, FF), D ** -0.5, 0.1875, ((0, 32),))
    w_up = centred(key_list[5], (EXPERTS, D, FF), D ** -0.5, 0.1875, ((0, 32),))
    w_down = centred(key_list[6], (EXPERTS, FF, D), FF ** -0.5, 0.3125, ((0, 32),))
    return dict(tokens=tokens, cotangent=cotangent, expert_ids=expert_ids, gate_probs=gate_probs, w_gate=w_gate, w_up=w_up, w_down=w_down)


def silu_parts(gate):
    sig = jax.nn.sigmoid(gate)
    return gate * sig, sig + gate * sig * (1.0 - sig)


def reference(tokens, cotangent, expert_ids, gate_probs, w_gate, w_up, w_down):
    blocks = TOKENS // TOK_DEV
    assigns = TOK_DEV * TOPK
    ids = expert_ids.reshape(blocks, assigns).astype(jnp.int32)
    onehot = (ids[:, :, None] == jnp.arange(EXPERTS, dtype=jnp.int32)[None, None, :]).astype(jnp.int32)
    ranks = jnp.cumsum(onehot, axis=1) - 1
    slots = jnp.sum(ranks * onehot, axis=2).astype(jnp.int32)
    target = ids * MOST + slots
    base = jnp.arange(blocks, dtype=jnp.int32)[:, None] * assigns
    filled = jnp.full((blocks, EXPERTS * MOST), -1, jnp.int32)
    filled = filled.at[jnp.arange(blocks, dtype=jnp.int32)[:, None], target].set(base + jnp.arange(assigns, dtype=jnp.int32)[None, :])
    empty_slot = filled < 0
    tok_index = jnp.where(empty_slot, TOKENS, filled // TOPK).astype(jnp.int32)
    prob_index = jnp.where(empty_slot, TOKENS * TOPK, filled).astype(jnp.int32)
    span = N_EXPERT * MOST
    tok_index = tok_index.reshape(N_DP, N_EXPERT, EXPERTS, MOST).transpose(2, 0, 1, 3).reshape(EXPERTS, N_DP, span)
    prob_index = prob_index.reshape(N_DP, N_EXPERT, EXPERTS, MOST).transpose(2, 0, 1, 3).reshape(EXPERTS, N_DP, span)
    zero_row = jnp.zeros((1, D), jnp.bfloat16)
    x_ext = jnp.concatenate([tokens, zero_row], axis=0)
    dy_ext = jnp.concatenate([cotangent, zero_row], axis=0)
    p_ext = jnp.concatenate([gate_probs.reshape(TOKENS * TOPK), jnp.zeros((1,), jnp.bfloat16)], axis=0)

    def one_expert(carry, inputs):
        grad_acc, prob_acc = carry
        rows_tok, rows_prob, weight_gate, weight_up, weight_down = inputs

        def one_group(inner, idx):
            acc, sums = inner
            tok_idx, p_idx = idx
            xr = x_ext[tok_idx]
            dyr = dy_ext[tok_idx]
            prob = p_ext[p_idx].astype(jnp.float32)[:, None]
            gate = jnp.dot(xr, weight_gate, preferred_element_type=jnp.float32)
            up = jnp.dot(xr, weight_up, preferred_element_type=jnp.float32)
            act, dact = silu_parts(gate)
            hidden = (act * up).astype(jnp.bfloat16)
            dz = jnp.dot(dyr, weight_down.T, preferred_element_type=jnp.float32)
            gp = jnp.sum(dz * hidden.astype(jnp.float32), axis=1).astype(jnp.bfloat16)
            dh = prob * dz
            d_gate = (dh * up * dact).astype(jnp.bfloat16)
            d_up = (dh * act).astype(jnp.bfloat16)
            scaled = (prob * dyr.astype(jnp.float32)).astype(jnp.bfloat16)
            row_grad = (jnp.dot(d_gate, weight_gate.T, preferred_element_type=jnp.float32)
                        + jnp.dot(d_up, weight_up.T, preferred_element_type=jnp.float32)).astype(jnp.bfloat16)
            part_gate = jnp.dot(xr.T, d_gate, preferred_element_type=jnp.float32).astype(jnp.bfloat16)
            part_up = jnp.dot(xr.T, d_up, preferred_element_type=jnp.float32).astype(jnp.bfloat16)
            part_down = jnp.dot(hidden.T, scaled, preferred_element_type=jnp.float32).astype(jnp.bfloat16)
            sums = (sums[0] + part_gate.astype(jnp.float32), sums[1] + part_up.astype(jnp.float32),
                    sums[2] + part_down.astype(jnp.float32))
            acc = (acc[0].at[tok_idx].add(row_grad.astype(jnp.float32)),
                   acc[1].at[p_idx].add(gp.astype(jnp.float32)))
            return (acc, sums), None

        init = ((grad_acc, prob_acc),
                (jnp.zeros((D, FF), jnp.float32), jnp.zeros((D, FF), jnp.float32), jnp.zeros((FF, D), jnp.float32)))
        (acc, sums), unused = lax.scan(one_group, init, (rows_tok, rows_prob))
        return acc, (sums[0].astype(jnp.bfloat16), sums[1].astype(jnp.bfloat16), sums[2].astype(jnp.bfloat16))

    start = (jnp.zeros((TOKENS + 1, D), jnp.float32), jnp.zeros((TOKENS * TOPK + 1,), jnp.float32))
    (grad_acc, prob_acc), (grad_gate, grad_up, grad_down) = lax.scan(
        one_expert, start, (tok_index, prob_index, w_gate, w_up, w_down))
    grad_tokens = grad_acc[:TOKENS].astype(jnp.bfloat16)
    grad_probs = prob_acc[:TOKENS * TOPK].reshape(TOKENS, TOPK).astype(jnp.bfloat16)
    return (grad_tokens, grad_probs, grad_gate, grad_up, grad_down)
```

```python
import functools

import jax
import jax.numpy as jnp
from jax import lax
from jax.experimental import pallas as pl
from jax.experimental.pallas import tpu as pltpu
from jax.sharding import PartitionSpec as P

MESH = pl.DeviceIdType.MESH
F32 = jnp.float32
BF16 = jnp.bfloat16
LANES = 128
STEP = 256


def contract(a, b, on_a, on_b):
    return lax.dot_general(a, b, (((on_a,), (on_b,)), ((), ())), preferred_element_type=F32)


def kernel(
    ids_ref, probs_ref, x_ref, dy_ref, wg_ref, wu_ref, wd_ref,
    gt_ref, gp_ref, og_ref, ou_ref, od_ref,
    x_all, dy_all, p_all, rows, grows, rpart, gpart, land, gland,
    wgu, wd, acc_gu, acc_d, gu, dz, dgu, hp,
    stage_g, stage_d, land_g, land_d,
    ag_s, ag_r, pc_s, pc_r, rp_s, rp_r, rs_s, rs_r, g_s, g_r, w_s, w_r, loc,
):
    ndp, nex = lax.axis_size("dp"), lax.axis_size("expert")
    me_dp, me = lax.axis_index("dp"), lax.axis_index("expert")
    steps = nex // 4
    tok, width = gt_ref.shape
    half = tok // 2
    ff = wd.shape[0]
    experts = p_all.shape[1]
    topk = ids_ref.shape[1]
    cut_g, cut_d = width // ndp, ff // ndp
    right = (me_dp, lax.rem(me + 2, nex))
    left = (me_dp, lax.rem(me + nex - 2, nex))
    partner = (me_dp, me + 1 - 2 * lax.rem(me, 2))
    toward = (right, left)
    peers = [(lax.rem(me_dp + j, ndp), me) for j in range(1, ndp)]

    def send(src, dst, ssem, rsem, dev):
        return pltpu.make_async_remote_copy(
            src_ref=src, dst_ref=dst, send_sem=ssem, recv_sem=rsem, device_id=dev, device_id_type=MESH
        )

    barrier = pltpu.get_barrier_semaphore()
    for dev in [right, left, partner] + peers:
        pl.semaphore_signal(barrier, inc=1, device_id=dev, device_id_type=MESH)
    local = [
        pltpu.make_async_copy(x_ref, x_all.at[0], loc.at[0]),
        pltpu.make_async_copy(dy_ref, dy_all.at[0], loc.at[1]),
        pltpu.make_async_copy(wg_ref.at[0], wgu.at[:, pl.ds(0, ff)], loc.at[2]),
        pltpu.make_async_copy(wu_ref.at[0], wgu.at[:, pl.ds(ff, ff)], loc.at[3]),
        pltpu.make_async_copy(wd_ref.at[0], wd, loc.at[4]),
    ]
    for copy in local:
        copy.start()
    pl.semaphore_wait(barrier, 3 + len(peers))

    streams = (x_all, dy_all)

    def own_slot(s, way):
        return 4 * s - 2 + way

    for k, src in ((0, x_ref), (1, dy_ref)):
        for way in range(2):
            send(src, streams[k].at[own_slot(1, way)], ag_s.at[k, 1, way], ag_r.at[k, 1, way], toward[way]).start()
        send(src, streams[k].at[1], pc_s.at[k, 0, 0], pc_r.at[k, 0, 0], partner).start()

    lane = lax.broadcasted_iota(jnp.int32, (tok, LANES), 1)
    table = jnp.zeros((tok, LANES), F32)
    for k in range(topk):
        table = jnp.where(lane == ids_ref[:, k : k + 1], probs_ref[:, k : k + 1].astype(F32), table)
    p_all[0] = table.T[:experts].astype(BF16)
    acc_gu[...] = jnp.zeros_like(acc_gu)
    acc_d[...] = jnp.zeros_like(acc_d)
    for way in range(2):
        send(p_all.at[0], p_all.at[own_slot(1, way)], ag_s.at[2, 1, way], ag_r.at[2, 1, way], toward[way]).start()
    send(p_all.at[0], p_all.at[1], pc_s.at[2, 0, 0], pc_r.at[2, 0, 0], partner).start()
    for copy in local:
        copy.wait()

    def part(way):
        return pl.ds(way * half, half)

    def full_in(k, ref, s, way):
        at = ref.at[own_slot(s, way)]
        return send(at, at, ag_s.at[k, s, way], ag_r.at[k, s, way], toward[way])

    def cross(k, ref, s, way):
        return send(
            ref.at[own_slot(s, way)], ref.at[4 * s + way], pc_s.at[k, s, way], pc_r.at[k, s, way], partner
        )

    def forward(k, ref, s, way):
        return send(
            ref.at[own_slot(s, way)], ref.at[own_slot(s + 1, way)],
            ag_s.at[k, s + 1, way], ag_r.at[k, s + 1, way], toward[way],
        )

    last_own, last_cross = 4 * steps - 2, 4 * steps - 1

    def forward_half(k, ref, way):
        return send(
            ref.at[own_slot(steps - 1, way), part(way)], ref.at[last_own, part(way)],
            ag_s.at[k, steps, way], ag_r.at[k, steps, way], toward[way],
        )

    def cross_half(k, ref, way):
        return send(
            ref.at[last_own, part(way)], ref.at[last_cross, part(way)],
            pc_s.at[k, steps, way], pc_r.at[k, steps, way], partner,
        )

    def forward_p_last():
        return send(
            p_all.at[own_slot(steps - 1, 0)], p_all.at[last_own],
            ag_s.at[2, steps, 0], ag_r.at[2, steps, 0], right,
        )

    def cross_p_last():
        return send(
            p_all.at[last_own], p_all.at[last_cross], pc_s.at[2, steps, 0], pc_r.at[2, steps, 0], partner
        )

    def poll(k, s):
        ref = streams[k]

        @pl.when(s < steps)
        def _():
            for way in range(2):
                full_in(k, ref, s, way).wait_recv()

                @pl.when(s < steps - 1)
                def _():
                    forward(k, ref, s, way).start()

                @pl.when(s == steps - 1)
                def _():
                    forward_half(k, ref, way).start()

                cross(k, ref, s, way).start()
            if k == 1:
                for way in range(2):
                    full_in(2, p_all, s, way).wait_recv()

                    @pl.when(s < steps - 1)
                    def _():
                        forward(2, p_all, s, way).start()

                    cross(2, p_all, s, way).start()

                @pl.when(s == steps - 1)
                def _():
                    forward_p_last().start()

        @pl.when(s == steps)
        def _():
            for way in range(2):
                forward_half(k, ref, way).wait_recv()
                cross_half(k, ref, way).start()
            if k == 1:
                forward_p_last().wait_recv()
                cross_p_last().start()

    def rows_out(i):
        return (
            send(rows.at[pl.ds(4 * i, 2)], rpart.at[pl.ds(2 * i - 1, 2)], rp_s.at[0, i], rp_r.at[0, i], partner),
            send(grows.at[pl.ds(4 * i, 2)], gpart.at[pl.ds(2 * i - 1, 2)], rp_s.at[1, i], rp_r.at[1, i], partner),
        )

    def rows_first():
        return (
            send(rows.at[1], rpart.at[0], rp_s.at[0, 0], rp_r.at[0, 0], partner),
            send(grows.at[1], gpart.at[0], rp_s.at[1, 0], rp_r.at[1, 0], partner),
        )

    def rows_last():
        return (
            send(rows.at[last_cross], rpart.at[2 * steps - 1], rp_s.at[0, steps], rp_r.at[0, steps], partner),
            send(grows.at[last_cross], gpart.at[2 * steps - 1], rp_s.at[1, steps], rp_r.at[1, steps], partner),
        )

    wide = 2 * tok
    pick = (lax.broadcasted_iota(jnp.int32, (experts, LANES), 0) == me).astype(F32).astype(BF16)

    def compute(u):
        at = pl.ds(2 * u, 2)
        for n in range(2 * ff // STEP):
            cols = pl.ds(n * STEP, STEP)
            gu[:, cols] = jnp.dot(
                x_all[at].reshape(wide, width), wgu[:, cols], preferred_element_type=F32
            )
        dz[...] = contract(dy_all[at].reshape(wide, width), wd[...], 1, 1)
        for b in range(2):
            prob = contract(p_all[2 * u + b], pick, 0, 0)
            gcol = []
            for r in range(0, tok, 32):
                chunk = pl.ds(b * tok + r, 32)
                pr = jnp.concatenate([prob[r : r + 32]] * (ff // LANES), axis=1)
                gate, up, back = gu[chunk, :ff], gu[chunk, ff:], dz[chunk, :]
                sig = jax.nn.sigmoid(gate)
                act = gate * sig
                hid = act * up
                gcol.append(jnp.sum(back * hid.astype(BF16).astype(F32), axis=1, keepdims=True))
                dh = pr * back
                dgu[chunk, :ff] = (dh * up * (sig + act * (1.0 - sig))).astype(BF16)
                dgu[chunk, ff:] = (dh * act).astype(BF16)
                hp[chunk, :] = (pr * hid).astype(BF16)
            column = jnp.concatenate(gcol, axis=0)
            grows[2 * u + b] = jnp.where(lane == me, column, 0.0).T[:experts].astype(BF16)
        for n in range(width // STEP):
            cols = pl.ds(n * STEP, STEP)
            rows[at, :, cols] = contract(dgu[...], wgu[cols, :], 1, 1).astype(BF16).reshape(2, tok, STEP)
        for n in range(width // STEP):
            cols = pl.ds(n * STEP, STEP)
            acc_gu[cols, :] += contract(x_all[at, :, cols].reshape(wide, STEP), dgu[...], 0, 0)
        for n in range(width // STEP):
            cols = pl.ds(n * STEP, STEP)
            acc_d[:, cols] += contract(hp[...], dy_all[at, :, cols].reshape(wide, STEP), 0, 0)

    def rs_copy(d, way, chunk, slot):
        return send(
            rows.at[slot, part(chunk)], land.at[way, d - 1, part(chunk)],
            rs_s.at[way, chunk, d - 1], rs_r.at[way, chunk, d - 1], toward[way],
        )

    def g_copy(d, way, slot):
        return send(
            grows.at[slot], gland.at[way, d - 1], g_s.at[way, d - 1], g_r.at[way, d - 1], toward[way]
        )

    def rs_flow(d, way, chunk, slot, other, first):
        lines = part(chunk)
        if not first:
            rs_copy(d + 1, way, chunk, slot).wait_recv()
        for r in range(0, half, 16):
            some = pl.ds(chunk * half + r, 16)
            total = rows[slot, some].astype(F32) + rpart[other, some].astype(F32)
            if not first:
                total = total + land[way, d, some].astype(F32)
            rows[slot, some] = total.astype(BF16)
        rs_copy(d, way, chunk, slot).start()
        if chunk == 0:
            if not first:
                g_copy(d + 1, way, slot).wait_recv()
            gsum = grows[slot].astype(F32) + gpart[other].astype(F32)
            if not first:
                gsum = gsum + gland[way, d].astype(F32)
            grows[slot] = gsum.astype(BF16)
            g_copy(d, way, slot).start()

    def near(d, way):
        return own_slot(d, 1 - way), 2 * d - way

    def unit(u, carry):
        i = u // 2
        even = lax.rem(u, 2) == 0

        @pl.when(u == 1)
        def _():
            poll(0, 1)

        @pl.when(jnp.logical_and(even, u > 0))
        def _():
            poll(0, i + 1)

        @pl.when(jnp.logical_not(even))
        def _():
            poll(1, i + 1)

        @pl.when(u == 0)
        def _():
            for k, ref in ((0, x_all), (1, dy_all), (2, p_all)):
                send(ref.at[0], ref.at[1], pc_s.at[k, 0, 0], pc_r.at[k, 0, 0], partner).wait_recv()

        @pl.when(jnp.logical_and(even, u > 0))
        def _():
            for k, ref in ((0, x_all), (1, dy_all), (2, p_all)):
                for way in range(2):
                    cross(k, ref, i, way).wait_recv()

        @pl.when(u == 2 * steps - 1)
        def _():
            for copy in rows_out(steps - 1):
                copy.wait_recv()
            for way in range(2):
                slot, other = near(steps - 1, way)
                rs_flow(steps - 1, way, 1 - way, slot, other, True)
            for way in range(2):
                cross_half(0, x_all, way).wait_recv()
                cross_half(1, dy_all, way).wait_recv()
            cross_p_last().wait_recv()

        compute(u)

        @pl.when(u == 0)
        def _():
            for copy in rows_first():
                copy.start()

        @pl.when(jnp.logical_and(even, u > 0))
        def _():
            for copy in rows_out(i):
                copy.start()

        @pl.when(u == 2 * steps - 1)
        def _():
            for copy in rows_last():
                copy.start()

        return carry

    lax.fori_loop(0, 2 * steps, unit, 0)

    for copy in rows_last():
        copy.wait_recv()
    for way in range(2):
        rs_flow(steps, way, way, last_own, 2 * steps - 1, True)

    def w_copies(j):
        to = lax.rem(me_dp + j, ndp)
        return (
            send(stage_g.at[to], land_g.at[j], w_s.at[0, j], w_r.at[0, j], (to, me)),
            send(stage_d.at[to], land_d.at[j], w_s.at[1, j], w_r.at[1, j], (to, me)),
        )

    for n in range(ndp):
        stage_g[n] = acc_gu[n * cut_g : (n + 1) * cut_g, :].astype(BF16)
    for n in range(ndp):
        stage_d[n] = acc_d[n * cut_d : (n + 1) * cut_d, :].astype(BF16)
    for j in range(1, ndp):
        for copy in w_copies(j):
            copy.start()

    def ring(t, carry):
        d = steps - 1 - t
        for way in range(2):
            slot, other = near(d, way)
            rs_flow(d, way, way, slot, other, False)

        @pl.when(d >= 2)
        def _():
            rp_wait = rows_out(d - 1)
            for copy in rp_wait:
                copy.wait_recv()
            for way in range(2):
                slot, other = near(d - 1, way)
                rs_flow(d - 1, way, 1 - way, slot, other, False)

        return carry

    lax.fori_loop(0, steps - 1, ring, 0)

    for copy in rows_first():
        copy.wait_recv()
    for way in range(2):
        rs_copy(1, way, 1 - way, 0).wait_recv()
    for way in range(2):
        rs_copy(1, way, way, 0).wait_recv()
        g_copy(1, way, 0).wait_recv()
    for r in range(0, tok, 16):
        some = pl.ds(r, 16)
        total = rows[0, some].astype(F32) + rpart[0, some].astype(F32)
        total = total + land[0, 0, some].astype(F32) + land[1, 0, some].astype(F32)
        gt_ref[some, :] = total.astype(BF16)
    gsum = grows[0].astype(F32) + gpart[0].astype(F32) + gland[0, 0].astype(F32) + gland[1, 0].astype(F32)
    if experts < LANES:
        gsum = jnp.concatenate([gsum, jnp.zeros((LANES - experts, tok), F32)], axis=0)
    gtab = gsum.T
    picked = []
    for k in range(topk):
        picked.append(
            jnp.sum(jnp.where(lane == ids_ref[:, k : k + 1], gtab, 0.0), axis=1, keepdims=True)
        )
    gp_ref[...] = jnp.concatenate(picked, axis=1).astype(BF16)

    for j in range(1, ndp):
        for copy in w_copies(j):
            copy.wait_recv()
    sum_g = stage_g[me_dp].astype(F32)
    sum_d = stage_d[me_dp].astype(F32)
    for j in range(1, ndp):
        sum_g = sum_g + land_g[j].astype(F32)
        sum_d = sum_d + land_d[j].astype(F32)
    og_ref[0] = sum_g[:, :ff].astype(BF16)
    ou_ref[0] = sum_g[:, ff:].astype(BF16)
    od_ref[0] = sum_d.astype(BF16)

    for k, src in ((0, x_ref), (1, dy_ref), (2, p_all.at[0])):
        ref = (x_all, dy_all, p_all)[k]
        for way in range(2):
            send(src, ref.at[own_slot(1, way)], ag_s.at[k, 1, way], ag_r.at[k, 1, way], toward[way]).wait_send()
        send(src, ref.at[1], pc_s.at[k, 0, 0], pc_r.at[k, 0, 0], partner).wait_send()

    def drain(s, carry):
        for k, ref in ((0, x_all), (1, dy_all), (2, p_all)):
            for way in range(2):
                cross(k, ref, s, way).wait_send()

                @pl.when(s < steps - 1)
                def _():
                    forward(k, ref, s, way).wait_send()

        for copy in rows_out(s):
            copy.wait_send()
        for way in range(2):
            slot, _ = near(s, way)
            for chunk in range(2):
                rs_copy(s, way, chunk, slot).wait_send()
            g_copy(s, way, slot).wait_send()
        return carry

    lax.fori_loop(1, steps, drain, 0)
    for k, ref in ((0, x_all), (1, dy_all)):
        for way in range(2):
            forward_half(k, ref, way).wait_send()
            cross_half(k, ref, way).wait_send()
    forward_p_last().wait_send()
    cross_p_last().wait_send()
    for copy in rows_first() + rows_last():
        copy.wait_send()
    for way in range(2):
        rs_copy(steps, way, way, last_own).wait_send()
    g_copy(steps, 0, last_own).wait_send()
    for j in range(1, ndp):
        for copy in w_copies(j):
            copy.wait_send()


def on_device(tokens, cotangent, expert_ids, gate_probs, w_gate, w_up, w_down):
    ndp, nex = lax.axis_size("dp"), lax.axis_size("expert")
    steps = nex // 4
    tok, width = tokens.shape
    ff = w_gate.shape[2]
    topk = expert_ids.shape[1]
    cut_g, cut_d = width // ndp, ff // ndp
    blocks = 4 * steps
    vmem = pl.BlockSpec(memory_space=pltpu.VMEM)
    hbm = pl.BlockSpec(memory_space=pl.ANY)
    dma = pltpu.SemaphoreType.DMA
    return pl.pallas_call(
        kernel,
        out_shape=(
            jax.ShapeDtypeStruct((tok, width), BF16),
            jax.ShapeDtypeStruct((tok, topk), BF16),
            jax.ShapeDtypeStruct((1, cut_g, ff), BF16),
            jax.ShapeDtypeStruct((1, cut_g, ff), BF16),
            jax.ShapeDtypeStruct((1, cut_d, width), BF16),
        ),
        in_specs=[vmem, vmem, hbm, hbm, hbm, hbm, hbm],
        out_specs=[vmem] * 5,
        scratch_shapes=[
            pltpu.VMEM((blocks, tok, width), BF16),
            pltpu.VMEM((blocks, tok, width), BF16),
            pltpu.VMEM((blocks, nex, tok), BF16),
            pltpu.VMEM((blocks, tok, width), BF16),
            pltpu.VMEM((blocks, nex, tok), BF16),
            pltpu.VMEM((blocks // 2, tok, width), BF16),
            pltpu.VMEM((blocks // 2, nex, tok), BF16),
            pltpu.VMEM((2, steps, tok, width), BF16),
            pltpu.VMEM((2, steps, nex, tok), BF16),
            pltpu.VMEM((width, 2 * ff), BF16),
            pltpu.VMEM((ff, width), BF16),
            pltpu.VMEM((width, 2 * ff), F32),
            pltpu.VMEM((ff, width), F32),
            pltpu.VMEM((2 * tok, 2 * ff), F32),
            pltpu.VMEM((2 * tok, ff), F32),
            pltpu.VMEM((2 * tok, 2 * ff), BF16),
            pltpu.VMEM((2 * tok, ff), BF16),
            pltpu.VMEM((ndp, cut_g, 2 * ff), BF16),
            pltpu.VMEM((ndp, cut_d, width), BF16),
            pltpu.VMEM((ndp, cut_g, 2 * ff), BF16),
            pltpu.VMEM((ndp, cut_d, width), BF16),
            dma((3, steps + 1, 2)),
            dma((3, steps + 1, 2)),
            dma((3, steps + 1, 2)),
            dma((3, steps + 1, 2)),
            dma((2, steps + 1)),
            dma((2, steps + 1)),
            dma((2, 2, steps)),
            dma((2, 2, steps)),
            dma((2, steps)),
            dma((2, steps)),
            dma((2, ndp)),
            dma((2, ndp)),
            dma((5,)),
        ],
        compiler_params=pltpu.CompilerParams(
            collective_id=0, has_side_effects=True, vmem_limit_bytes=63 * 1024 * 1024
        ),
        name="moe_backward",
    )(expert_ids, gate_probs, tokens, cotangent, w_gate, w_up, w_down)


def solution(mesh):
    return jax.shard_map(
        on_device,
        mesh=mesh,
        in_specs=(
            P(("dp", "expert"), None),
            P(("dp", "expert"), None),
            P(("dp", "expert"), None),
            P(("dp", "expert"), None),
            P("expert", None, None),
            P("expert", None, None),
            P("expert", None, None),
        ),
        out_specs=(
            P(("dp", "expert"), None),
            P(("dp", "expert"), None),
            P("expert", "dp", None),
            P("expert", "dp", None),
            P("expert", "dp", None),
        ),
        check_vma=False,
    )
```

```python
import functools

import jax
import jax.numpy as jnp
from jax import lax
from jax.experimental import pallas as pl
from jax.experimental.pallas import tpu as pltpu
from jax.sharding import PartitionSpec as P

MESH = pl.DeviceIdType.MESH
F32 = jnp.float32
BF16 = jnp.bfloat16
LANES = 128
STEP = 256


def contract(a, b, on_a, on_b):
    return lax.dot_general(a, b, (((on_a,), (on_b,)), ((), ())), preferred_element_type=F32)


def kernel(
    ids_ref, probs_ref, x_ref, dy_ref, wg_ref, wu_ref, wd_ref,
    gt_ref, gp_ref, og_ref, ou_ref, od_ref,
    x_all, dy_all, p_all, rows, grows, rpart, gpart, land, gland,
    wgu, wd, acc_gu, acc_d, gu, dz, dgu, hp,
    stage_g, stage_d, land_g, land_d,
    ag_s, ag_r, pc_s, pc_r, rp_s, rp_r, rs_s, rs_r, g_s, g_r, w_s, w_r, loc,
):
    ndp, nex = lax.axis_size("dp"), lax.axis_size("expert")
    me_dp, me = lax.axis_index("dp"), lax.axis_index("expert")
    steps = nex // 4
    tok, width = gt_ref.shape
    half = tok // 2
    ff = wd.shape[0]
    experts = p_all.shape[1]
    topk = ids_ref.shape[0]
    cut_g, cut_d = width // ndp, ff // ndp
    right = (me_dp, lax.rem(me + 2, nex))
    left = (me_dp, lax.rem(me + nex - 2, nex))
    partner = (me_dp, me + 1 - 2 * lax.rem(me, 2))
    toward = (right, left)
    peers = [(lax.rem(me_dp + j, ndp), me) for j in range(1, ndp)]

    def send(src, dst, ssem, rsem, dev):
        return pltpu.make_async_remote_copy(
            src_ref=src, dst_ref=dst, send_sem=ssem, recv_sem=rsem, device_id=dev, device_id_type=MESH
        )

    barrier = pltpu.get_barrier_semaphore()
    for dev in [right, left, partner] + peers:
        pl.semaphore_signal(barrier, inc=1, device_id=dev, device_id_type=MESH)
    local = [
        pltpu.make_async_copy(x_ref, x_all.at[0], loc.at[0]),
        pltpu.make_async_copy(dy_ref, dy_all.at[0], loc.at[1]),
        pltpu.make_async_copy(wg_ref.at[0], wgu.at[:, pl.ds(0, ff)], loc.at[2]),
        pltpu.make_async_copy(wu_ref.at[0], wgu.at[:, pl.ds(ff, ff)], loc.at[3]),
        pltpu.make_async_copy(wd_ref.at[0], wd, loc.at[4]),
    ]
    for copy in local:
        copy.start()
    pl.semaphore_wait(barrier, 3 + len(peers))

    streams = (x_all, dy_all)

    def own_slot(s, way):
        return 4 * s - 2 + way

    for k, src in ((0, x_ref), (1, dy_ref)):
        for way in range(2):
            send(src, streams[k].at[own_slot(1, way)], ag_s.at[k, 1, way], ag_r.at[k, 1, way], toward[way]).start()
        send(src, streams[k].at[1], pc_s.at[k, 0, 0], pc_r.at[k, 0, 0], partner).start()

    lane = lax.broadcasted_iota(jnp.int32, (tok, LANES), 1)
    line = lax.broadcasted_iota(jnp.int32, (experts, tok), 0)
    table = jnp.zeros((experts, tok), F32)
    for k in range(topk):
        table = jnp.where(line == ids_ref[k : k + 1, :], probs_ref[k : k + 1, :].astype(F32), table)
    p_all[0] = table.astype(BF16)
    acc_gu[...] = jnp.zeros_like(acc_gu)
    acc_d[...] = jnp.zeros_like(acc_d)
    for way in range(2):
        send(p_all.at[0], p_all.at[own_slot(1, way)], ag_s.at[2, 1, way], ag_r.at[2, 1, way], toward[way]).start()
    send(p_all.at[0], p_all.at[1], pc_s.at[2, 0, 0], pc_r.at[2, 0, 0], partner).start()
    for copy in local:
        copy.wait()

    def part(way):
        return pl.ds(way * half, half)

    def full_in(k, ref, s, way):
        at = ref.at[own_slot(s, way)]
        return send(at, at, ag_s.at[k, s, way], ag_r.at[k, s, way], toward[way])

    def cross(k, ref, s, way):
        return send(
            ref.at[own_slot(s, way)], ref.at[4 * s + way], pc_s.at[k, s, way], pc_r.at[k, s, way], partner
        )

    def forward(k, ref, s, way):
        return send(
            ref.at[own_slot(s, way)], ref.at[own_slot(s + 1, way)],
            ag_s.at[k, s + 1, way], ag_r.at[k, s + 1, way], toward[way],
        )

    last_own, last_cross = 4 * steps - 2, 4 * steps - 1

    def forward_half(k, ref, way):
        return send(
            ref.at[own_slot(steps - 1, way), part(way)], ref.at[last_own, part(way)],
            ag_s.at[k, steps, way], ag_r.at[k, steps, way], toward[way],
        )

    def cross_half(k, ref, way):
        return send(
            ref.at[last_own, part(way)], ref.at[last_cross, part(way)],
            pc_s.at[k, steps, way], pc_r.at[k, steps, way], partner,
        )

    def forward_p_last():
        return send(
            p_all.at[own_slot(steps - 1, 0)], p_all.at[last_own],
            ag_s.at[2, steps, 0], ag_r.at[2, steps, 0], right,
        )

    def cross_p_last():
        return send(
            p_all.at[last_own], p_all.at[last_cross], pc_s.at[2, steps, 0], pc_r.at[2, steps, 0], partner
        )

    def poll(k, s):
        ref = streams[k]

        @pl.when(s < steps)
        def _():
            for way in range(2):
                full_in(k, ref, s, way).wait_recv()

                @pl.when(s < steps - 1)
                def _():
                    forward(k, ref, s, way).start()

                @pl.when(s == steps - 1)
                def _():
                    forward_half(k, ref, way).start()

                cross(k, ref, s, way).start()
            if k == 1:
                for way in range(2):
                    full_in(2, p_all, s, way).wait_recv()

                    @pl.when(s < steps - 1)
                    def _():
                        forward(2, p_all, s, way).start()

                    cross(2, p_all, s, way).start()

                @pl.when(s == steps - 1)
                def _():
                    forward_p_last().start()

        @pl.when(s == steps)
        def _():
            for way in range(2):
                forward_half(k, ref, way).wait_recv()
                cross_half(k, ref, way).start()
            if k == 1:
                forward_p_last().wait_recv()
                cross_p_last().start()

    def rows_out(i):
        return (
            send(rows.at[pl.ds(4 * i, 2)], rpart.at[pl.ds(2 * i - 1, 2)], rp_s.at[0, i], rp_r.at[0, i], partner),
            send(grows.at[pl.ds(4 * i, 2)], gpart.at[pl.ds(2 * i - 1, 2)], rp_s.at[1, i], rp_r.at[1, i], partner),
        )

    def rows_first():
        return (
            send(rows.at[1], rpart.at[0], rp_s.at[0, 0], rp_r.at[0, 0], partner),
            send(grows.at[1], gpart.at[0], rp_s.at[1, 0], rp_r.at[1, 0], partner),
        )

    def rows_last():
        return (
            send(rows.at[last_cross], rpart.at[2 * steps - 1], rp_s.at[0, steps], rp_r.at[0, steps], partner),
            send(grows.at[last_cross], gpart.at[2 * steps - 1], rp_s.at[1, steps], rp_r.at[1, steps], partner),
        )

    wide = 2 * tok
    pick = (lax.broadcasted_iota(jnp.int32, (experts, LANES), 0) == me).astype(F32).astype(BF16)

    def compute(u):
        at = pl.ds(2 * u, 2)
        for n in range(2 * ff // STEP):
            cols = pl.ds(n * STEP, STEP)
            gu[:, cols] = jnp.dot(
                x_all[at].reshape(wide, width), wgu[:, cols], preferred_element_type=F32
            )
        dz[...] = contract(dy_all[at].reshape(wide, width), wd[...], 1, 1)
        for b in range(2):
            prob = contract(p_all[2 * u + b], pick, 0, 0)
            gcol = []
            for r in range(0, tok, 32):
                chunk = pl.ds(b * tok + r, 32)
                pr = jnp.concatenate([prob[r : r + 32]] * (ff // LANES), axis=1)
                gate, up, back = gu[chunk, :ff], gu[chunk, ff:], dz[chunk, :]
                sig = jax.nn.sigmoid(gate)
                act = gate * sig
                hid = act * up
                gcol.append(jnp.sum(back * hid.astype(BF16).astype(F32), axis=1, keepdims=True))
                dh = pr * back
                dgu[chunk, :ff] = (dh * up * (sig + act * (1.0 - sig))).astype(BF16)
                dgu[chunk, ff:] = (dh * act).astype(BF16)
                hp[chunk, :] = (pr * hid).astype(BF16)
            column = jnp.concatenate(gcol, axis=0)
            grows[2 * u + b] = jnp.where(lane == me, column, 0.0).T[:experts].astype(BF16)
        for n in range(width // STEP):
            cols = pl.ds(n * STEP, STEP)
            rows[at, :, cols] = contract(dgu[...], wgu[cols, :], 1, 1).astype(BF16).reshape(2, tok, STEP)

    def gather_weights(u):
        at = pl.ds(2 * u, 2)
        for n in range(width // STEP):
            cols = pl.ds(n * STEP, STEP)
            acc_gu[cols, :] += contract(x_all[at, :, cols].reshape(wide, STEP), dgu[...], 0, 0)
        for n in range(width // STEP):
            cols = pl.ds(n * STEP, STEP)
            acc_d[:, cols] += contract(hp[...], dy_all[at, :, cols].reshape(wide, STEP), 0, 0)

    def rs_copy(d, way, chunk, slot):
        return send(
            rows.at[slot, part(chunk)], land.at[way, d - 1, part(chunk)],
            rs_s.at[way, chunk, d - 1], rs_r.at[way, chunk, d - 1], toward[way],
        )

    def g_copy(d, way, slot):
        return send(
            grows.at[slot], gland.at[way, d - 1], g_s.at[way, d - 1], g_r.at[way, d - 1], toward[way]
        )

    def rs_flow(d, way, chunk, slot, other, first):
        lines = part(chunk)
        if not first:
            rs_copy(d + 1, way, chunk, slot).wait_recv()
        for r in range(0, half, 16):
            some = pl.ds(chunk * half + r, 16)
            total = rows[slot, some].astype(F32) + rpart[other, some].astype(F32)
            if not first:
                total = total + land[way, d, some].astype(F32)
            rows[slot, some] = total.astype(BF16)
        rs_copy(d, way, chunk, slot).start()
        if chunk == 0:
            if not first:
                g_copy(d + 1, way, slot).wait_recv()
            gsum = grows[slot].astype(F32) + gpart[other].astype(F32)
            if not first:
                gsum = gsum + gland[way, d].astype(F32)
            grows[slot] = gsum.astype(BF16)
            g_copy(d, way, slot).start()

    def near(d, way):
        return own_slot(d, 1 - way), 2 * d - way

    def unit(u, carry):
        i = u // 2
        even = lax.rem(u, 2) == 0

        @pl.when(u == 1)
        def _():
            poll(0, 1)

        @pl.when(jnp.logical_and(even, u > 0))
        def _():
            poll(0, i + 1)

        @pl.when(jnp.logical_not(even))
        def _():
            poll(1, i + 1)

        @pl.when(u == 0)
        def _():
            for k, ref in ((0, x_all), (1, dy_all), (2, p_all)):
                send(ref.at[0], ref.at[1], pc_s.at[k, 0, 0], pc_r.at[k, 0, 0], partner).wait_recv()

        @pl.when(jnp.logical_and(even, u > 0))
        def _():
            for k, ref in ((0, x_all), (1, dy_all), (2, p_all)):
                for way in range(2):
                    cross(k, ref, i, way).wait_recv()

        @pl.when(u == 2 * steps - 1)
        def _():
            for copy in rows_out(steps - 1):
                copy.wait_recv()
            for way in range(2):
                slot, other = near(steps - 1, way)
                rs_flow(steps - 1, way, 1 - way, slot, other, True)
            for way in range(2):
                cross_half(0, x_all, way).wait_recv()
                cross_half(1, dy_all, way).wait_recv()
            cross_p_last().wait_recv()

        compute(u)

        @pl.when(u == 0)
        def _():
            for copy in rows_first():
                copy.start()

        @pl.when(jnp.logical_and(even, u > 0))
        def _():
            for copy in rows_out(i):
                copy.start()

        @pl.when(u == 2 * steps - 1)
        def _():
            for copy in rows_last():
                copy.start()

        gather_weights(u)
        return carry

    lax.fori_loop(0, 2 * steps, unit, 0)

    for copy in rows_last():
        copy.wait_recv()
    for way in range(2):
        rs_flow(steps, way, way, last_own, 2 * steps - 1, True)

    def w_copies(j):
        to = lax.rem(me_dp + j, ndp)
        return (
            send(stage_g.at[to], land_g.at[j], w_s.at[0, j], w_r.at[0, j], (to, me)),
            send(stage_d.at[to], land_d.at[j], w_s.at[1, j], w_r.at[1, j], (to, me)),
        )

    for n in range(ndp):
        stage_g[n] = acc_gu[n * cut_g : (n + 1) * cut_g, :].astype(BF16)
    for n in range(ndp):
        stage_d[n] = acc_d[n * cut_d : (n + 1) * cut_d, :].astype(BF16)
    for j in range(1, ndp):
        for copy in w_copies(j):
            copy.start()

    def ring(t, carry):
        d = steps - 1 - t
        for way in range(2):
            slot, other = near(d, way)
            rs_flow(d, way, way, slot, other, False)

        @pl.when(d >= 2)
        def _():
            rp_wait = rows_out(d - 1)
            for copy in rp_wait:
                copy.wait_recv()
            for way in range(2):
                slot, other = near(d - 1, way)
                rs_flow(d - 1, way, 1 - way, slot, other, False)

        return carry

    lax.fori_loop(0, steps - 1, ring, 0)

    for j in range(1, ndp):
        for copy in w_copies(j):
            copy.wait_recv()
    sum_g = stage_g[me_dp].astype(F32)
    sum_d = stage_d[me_dp].astype(F32)
    for j in range(1, ndp):
        sum_g = sum_g + land_g[j].astype(F32)
        sum_d = sum_d + land_d[j].astype(F32)
    og_ref[0] = sum_g[:, :ff].astype(BF16)
    ou_ref[0] = sum_g[:, ff:].astype(BF16)
    od_ref[0] = sum_d.astype(BF16)

    for copy in rows_first():
        copy.wait_recv()
    for way in range(2):
        rs_copy(1, way, 1 - way, 0).wait_recv()
    for way in range(2):
        rs_copy(1, way, way, 0).wait_recv()
        g_copy(1, way, 0).wait_recv()
    for r in range(0, tok, 16):
        some = pl.ds(r, 16)
        total = rows[0, some].astype(F32) + rpart[0, some].astype(F32)
        total = total + land[0, 0, some].astype(F32) + land[1, 0, some].astype(F32)
        gt_ref[some, :] = total.astype(BF16)
    gsum = grows[0].astype(F32) + gpart[0].astype(F32) + gland[0, 0].astype(F32) + gland[1, 0].astype(F32)
    picked = []
    for k in range(topk):
        picked.append(jnp.sum(jnp.where(line == ids_ref[k : k + 1, :], gsum, 0.0), axis=0, keepdims=True))
    gp_ref[...] = jnp.concatenate(picked, axis=0).astype(BF16)

    for k, src in ((0, x_ref), (1, dy_ref), (2, p_all.at[0])):
        ref = (x_all, dy_all, p_all)[k]
        for way in range(2):
            send(src, ref.at[own_slot(1, way)], ag_s.at[k, 1, way], ag_r.at[k, 1, way], toward[way]).wait_send()
        send(src, ref.at[1], pc_s.at[k, 0, 0], pc_r.at[k, 0, 0], partner).wait_send()

    def drain(s, carry):
        for k, ref in ((0, x_all), (1, dy_all), (2, p_all)):
            for way in range(2):
                cross(k, ref, s, way).wait_send()

                @pl.when(s < steps - 1)
                def _():
                    forward(k, ref, s, way).wait_send()

        for copy in rows_out(s):
            copy.wait_send()
        for way in range(2):
            slot, _ = near(s, way)
            for chunk in range(2):
                rs_copy(s, way, chunk, slot).wait_send()
            g_copy(s, way, slot).wait_send()
        return carry

    lax.fori_loop(1, steps, drain, 0)
    for k, ref in ((0, x_all), (1, dy_all)):
        for way in range(2):
            forward_half(k, ref, way).wait_send()
            cross_half(k, ref, way).wait_send()
    forward_p_last().wait_send()
    cross_p_last().wait_send()
    for copy in rows_first() + rows_last():
        copy.wait_send()
    for way in range(2):
        rs_copy(steps, way, way, last_own).wait_send()
    g_copy(steps, 0, last_own).wait_send()
    for j in range(1, ndp):
        for copy in w_copies(j):
            copy.wait_send()


def hand_on(*refs):
    for src, dst in zip(refs[:5], refs[5:]):
        dst[...] = src[...]


def on_device(tokens, cotangent, expert_ids, gate_probs, w_gate, w_up, w_down):
    ndp, nex = lax.axis_size("dp"), lax.axis_size("expert")
    steps = nex // 4
    tok, width = tokens.shape
    ff = w_gate.shape[2]
    topk = expert_ids.shape[1]
    cut_g, cut_d = width // ndp, ff // ndp
    blocks = 4 * steps
    vmem = pl.BlockSpec(memory_space=pltpu.VMEM)
    hbm = pl.BlockSpec(memory_space=pl.ANY)
    dma = pltpu.SemaphoreType.DMA
    outs = pl.pallas_call(
        kernel,
        out_shape=(
            jax.ShapeDtypeStruct((tok, width), BF16),
            jax.ShapeDtypeStruct((topk, tok), BF16),
            jax.ShapeDtypeStruct((1, cut_g, ff), BF16),
            jax.ShapeDtypeStruct((1, cut_g, ff), BF16),
            jax.ShapeDtypeStruct((1, cut_d, width), BF16),
        ),
        in_specs=[vmem, vmem, hbm, hbm, hbm, hbm, hbm],
        out_specs=[vmem] * 5,
        scratch_shapes=[
            pltpu.VMEM((blocks, tok, width), BF16),
            pltpu.VMEM((blocks, tok, width), BF16),
            pltpu.VMEM((blocks, nex, tok), BF16),
            pltpu.VMEM((blocks, tok, width), BF16),
            pltpu.VMEM((blocks, nex, tok), BF16),
            pltpu.VMEM((blocks // 2, tok, width), BF16),
            pltpu.VMEM((blocks // 2, nex, tok), BF16),
            pltpu.VMEM((2, steps, tok, width), BF16),
            pltpu.VMEM((2, steps, nex, tok), BF16),
            pltpu.VMEM((width, 2 * ff), BF16),
            pltpu.VMEM((ff, width), BF16),
            pltpu.VMEM((width, 2 * ff), F32),
            pltpu.VMEM((ff, width), F32),
            pltpu.VMEM((2 * tok, 2 * ff), F32),
            pltpu.VMEM((2 * tok, ff), F32),
            pltpu.VMEM((2 * tok, 2 * ff), BF16),
            pltpu.VMEM((2 * tok, ff), BF16),
            pltpu.VMEM((ndp, cut_g, 2 * ff), BF16),
            pltpu.VMEM((ndp, cut_d, width), BF16),
            pltpu.VMEM((ndp, cut_g, 2 * ff), BF16),
            pltpu.VMEM((ndp, cut_d, width), BF16),
            dma((3, steps + 1, 2)),
            dma((3, steps + 1, 2)),
            dma((3, steps + 1, 2)),
            dma((3, steps + 1, 2)),
            dma((2, steps + 1)),
            dma((2, steps + 1)),
            dma((2, 2, steps)),
            dma((2, 2, steps)),
            dma((2, steps)),
            dma((2, steps)),
            dma((2, ndp)),
            dma((2, ndp)),
            dma((5,)),
        ],
        compiler_params=pltpu.CompilerParams(
            collective_id=0, has_side_effects=True, vmem_limit_bytes=63 * 1024 * 1024
        ),
        name="moe_backward",
    )(expert_ids.T, gate_probs.T, tokens, cotangent, w_gate, w_up, w_down)
    outs = pl.pallas_call(
        hand_on,
        out_shape=[jax.ShapeDtypeStruct(v.shape, v.dtype) for v in outs],
        in_specs=[vmem] * 5,
        out_specs=[vmem] * 5,
        name="hand_on",
    )(*outs)
    return outs[0], outs[1].T, outs[2], outs[3], outs[4]


def solution(mesh):
    return jax.shard_map(
        on_device,
        mesh=mesh,
        in_specs=(
            P(("dp", "expert"), None),
            P(("dp", "expert"), None),
            P(("dp", "expert"), None),
            P(("dp", "expert"), None),
            P("expert", None, None),
            P("expert", None, None),
            P("expert", None, None),
        ),
        out_specs=(
            P(("dp", "expert"), None),
            P(("dp", "expert"), None),
            P("expert", "dp", None),
            P("expert", "dp", None),
            P("expert", "dp", None),
        ),
        check_vma=False,
    )
```

```python
import functools

import jax
import jax.numpy as jnp
from jax import lax
from jax.experimental import pallas as pl
from jax.experimental.pallas import tpu as pltpu
from jax.sharding import PartitionSpec as P

MESH = pl.DeviceIdType.MESH
F32 = jnp.float32
BF16 = jnp.bfloat16
LANES = 128
STEP = 256
SIDE = 4


def contract(a, b, on_a, on_b):
    return lax.dot_general(a, b, (((on_a,), (on_b,)), ((), ())), preferred_element_type=F32)


def kernel(
    ids_ref, probs_ref, x_ref, dy_ref, wg_ref, wu_ref, wd_ref,
    gt_ref, gp_ref, og_ref, ou_ref, od_ref,
    x_all, dy_all, p_all, rows, grows, rpart, gpart, land, gland,
    wgu, wd, acc_gu, acc_d, gu, dz, dgu, hp,
    stage_g, stage_d, land_g, land_d,
    ag_s, ag_r, pc_s, pc_r, rp_s, rp_r, rs_s, rs_r, g_s, g_r, w_s, w_r, loc, ready_sem,
):
    ndp, nex = lax.axis_size("dp"), lax.axis_size("expert")
    me_dp, me = lax.axis_index("dp"), lax.axis_index("expert")
    steps = nex // 4
    tok, width = gt_ref.shape
    half = tok // 2
    ff = wd.shape[0]
    experts = p_all.shape[1]
    topk = ids_ref.shape[0]
    cut_g, cut_d = width // ndp, ff // ndp
    right = (me_dp, lax.rem(me + 2, nex))
    left = (me_dp, lax.rem(me + nex - 2, nex))
    partner = (me_dp, me + 1 - 2 * lax.rem(me, 2))
    toward = (right, left)
    peers = [(lax.rem(me_dp + j, ndp), me) for j in range(1, ndp)]

    def send(src, dst, ssem, rsem, dev):
        return pltpu.make_async_remote_copy(
            src_ref=src, dst_ref=dst, send_sem=ssem, recv_sem=rsem, device_id=dev, device_id_type=MESH
        )

    barrier = pltpu.get_barrier_semaphore()
    for dev in (right, left, partner):
        pl.semaphore_signal(barrier, inc=1, device_id=dev, device_id_type=MESH)

    def turn(dp):
        return (jnp.minimum(dp // SIDE, 2) + jnp.minimum(lax.rem(dp, SIDE), 2)) * ndp + dp

    ahead = [turn(dev[0]) < turn(me_dp) for dev in peers]
    for dev, first in zip(peers, ahead):

        @pl.when(jnp.logical_not(first))
        def _():
            pl.semaphore_signal(barrier, inc=1, device_id=dev, device_id_type=MESH)

    n_ahead = sum([jnp.where(first, 1, 0) for first in ahead], jnp.int32(0))
    local = [
        pltpu.make_async_copy(x_ref, x_all.at[0], loc.at[0]),
        pltpu.make_async_copy(dy_ref, dy_all.at[0], loc.at[1]),
        pltpu.make_async_copy(wg_ref.at[0], wgu.at[:, pl.ds(0, ff)], loc.at[2]),
        pltpu.make_async_copy(wu_ref.at[0], wgu.at[:, pl.ds(ff, ff)], loc.at[3]),
        pltpu.make_async_copy(wd_ref.at[0], wd, loc.at[4]),
    ]
    for copy in local:
        copy.start()
    pl.semaphore_wait(barrier, 3 + n_ahead)

    streams = (x_all, dy_all)

    def own_slot(s, way):
        return 4 * s - 2 + way

    for k, src in ((0, x_ref), (1, dy_ref)):
        for way in range(2):
            send(src, streams[k].at[own_slot(1, way)], ag_s.at[k, 1, way], ag_r.at[k, 1, way], toward[way]).start()
        send(src, streams[k].at[1], pc_s.at[k, 0, 0], pc_r.at[k, 0, 0], partner).start()

    for dev, first in zip(peers, ahead):

        @pl.when(first)
        def _():
            pl.semaphore_signal(ready_sem, inc=1, device_id=dev, device_id_type=MESH)

    lane = lax.broadcasted_iota(jnp.int32, (tok, LANES), 1)
    line = lax.broadcasted_iota(jnp.int32, (experts, tok), 0)
    table = jnp.zeros((experts, tok), F32)
    for k in range(topk):
        table = jnp.where(line == ids_ref[k : k + 1, :], probs_ref[k : k + 1, :].astype(F32), table)
    p_all[0] = table.astype(BF16)
    acc_gu[...] = jnp.zeros_like(acc_gu)
    acc_d[...] = jnp.zeros_like(acc_d)
    for way in range(2):
        send(p_all.at[0], p_all.at[own_slot(1, way)], ag_s.at[2, 1, way], ag_r.at[2, 1, way], toward[way]).start()
    send(p_all.at[0], p_all.at[1], pc_s.at[2, 0, 0], pc_r.at[2, 0, 0], partner).start()
    for copy in local:
        copy.wait()

    def part(way):
        return pl.ds(way * half, half)

    def full_in(k, ref, s, way):
        at = ref.at[own_slot(s, way)]
        return send(at, at, ag_s.at[k, s, way], ag_r.at[k, s, way], toward[way])

    def cross(k, ref, s, way):
        return send(
            ref.at[own_slot(s, way)], ref.at[4 * s + way], pc_s.at[k, s, way], pc_r.at[k, s, way], partner
        )

    def forward(k, ref, s, way):
        return send(
            ref.at[own_slot(s, way)], ref.at[own_slot(s + 1, way)],
            ag_s.at[k, s + 1, way], ag_r.at[k, s + 1, way], toward[way],
        )

    last_own, last_cross = 4 * steps - 2, 4 * steps - 1

    def forward_half(k, ref, way):
        return send(
            ref.at[own_slot(steps - 1, way), part(way)], ref.at[last_own, part(way)],
            ag_s.at[k, steps, way], ag_r.at[k, steps, way], toward[way],
        )

    def cross_half(k, ref, way):
        return send(
            ref.at[last_own, part(way)], ref.at[last_cross, part(way)],
            pc_s.at[k, steps, way], pc_r.at[k, steps, way], partner,
        )

    def forward_p_last():
        return send(
            p_all.at[own_slot(steps - 1, 0)], p_all.at[last_own],
            ag_s.at[2, steps, 0], ag_r.at[2, steps, 0], right,
        )

    def cross_p_last():
        return send(
            p_all.at[last_own], p_all.at[last_cross], pc_s.at[2, steps, 0], pc_r.at[2, steps, 0], partner
        )

    def poll(k, s):
        ref = streams[k]

        @pl.when(s < steps)
        def _():
            for way in range(2):
                full_in(k, ref, s, way).wait_recv()

                @pl.when(s < steps - 1)
                def _():
                    forward(k, ref, s, way).start()

                @pl.when(s == steps - 1)
                def _():
                    forward_half(k, ref, way).start()

                cross(k, ref, s, way).start()
            if k == 1:
                for way in range(2):
                    full_in(2, p_all, s, way).wait_recv()

                    @pl.when(s < steps - 1)
                    def _():
                        forward(2, p_all, s, way).start()

                    cross(2, p_all, s, way).start()

                @pl.when(s == steps - 1)
                def _():
                    forward_p_last().start()

        @pl.when(s == steps)
        def _():
            for way in range(2):
                forward_half(k, ref, way).wait_recv()
                cross_half(k, ref, way).start()
            if k == 1:
                forward_p_last().wait_recv()
                cross_p_last().start()

    def rows_out(i):
        return (
            send(rows.at[pl.ds(4 * i, 2)], rpart.at[pl.ds(2 * i - 1, 2)], rp_s.at[0, i], rp_r.at[0, i], partner),
            send(grows.at[pl.ds(4 * i, 2)], gpart.at[pl.ds(2 * i - 1, 2)], rp_s.at[1, i], rp_r.at[1, i], partner),
        )

    def rows_first():
        return (
            send(rows.at[1], rpart.at[0], rp_s.at[0, 0], rp_r.at[0, 0], partner),
            send(grows.at[1], gpart.at[0], rp_s.at[1, 0], rp_r.at[1, 0], partner),
        )

    def rows_last():
        return (
            send(rows.at[last_cross], rpart.at[2 * steps - 1], rp_s.at[0, steps], rp_r.at[0, steps], partner),
            send(grows.at[last_cross], gpart.at[2 * steps - 1], rp_s.at[1, steps], rp_r.at[1, steps], partner),
        )

    wide = 2 * tok
    pick = (lax.broadcasted_iota(jnp.int32, (experts, LANES), 0) == me).astype(F32).astype(BF16)

    def compute(u):
        at = pl.ds(2 * u, 2)
        for n in range(2 * ff // STEP):
            cols = pl.ds(n * STEP, STEP)
            gu[:, cols] = jnp.dot(
                x_all[at].reshape(wide, width), wgu[:, cols], preferred_element_type=F32
            )
        dz[...] = contract(dy_all[at].reshape(wide, width), wd[...], 1, 1)
        for b in range(2):
            prob = contract(p_all[2 * u + b], pick, 0, 0)
            gcol = []
            for r in range(0, tok, 32):
                chunk = pl.ds(b * tok + r, 32)
                pr = jnp.concatenate([prob[r : r + 32]] * (ff // LANES), axis=1)
                gate, up, back = gu[chunk, :ff], gu[chunk, ff:], dz[chunk, :]
                sig = jax.nn.sigmoid(gate)
                act = gate * sig
                hid = act * up
                gcol.append(jnp.sum(back * hid.astype(BF16).astype(F32), axis=1, keepdims=True))
                dh = pr * back
                dgu[chunk, :ff] = (dh * up * (sig + act * (1.0 - sig))).astype(BF16)
                dgu[chunk, ff:] = (dh * act).astype(BF16)
                hp[chunk, :] = (pr * hid).astype(BF16)
            column = jnp.concatenate(gcol, axis=0)
            grows[2 * u + b] = jnp.where(lane == me, column, 0.0).T[:experts].astype(BF16)
        for n in range(width // STEP):
            cols = pl.ds(n * STEP, STEP)
            rows[at, :, cols] = contract(dgu[...], wgu[cols, :], 1, 1).astype(BF16).reshape(2, tok, STEP)

    def gather_weights(u):
        at = pl.ds(2 * u, 2)
        for n in range(width // STEP):
            cols = pl.ds(n * STEP, STEP)
            acc_gu[cols, :] += contract(x_all[at, :, cols].reshape(wide, STEP), dgu[...], 0, 0)
        for n in range(width // STEP):
            cols = pl.ds(n * STEP, STEP)
            acc_d[:, cols] += contract(hp[...], dy_all[at, :, cols].reshape(wide, STEP), 0, 0)

    def rs_copy(d, way, chunk, slot):
        return send(
            rows.at[slot, part(chunk)], land.at[way, d - 1, part(chunk)],
            rs_s.at[way, chunk, d - 1], rs_r.at[way, chunk, d - 1], toward[way],
        )

    def g_copy(d, way, slot):
        return send(
            grows.at[slot], gland.at[way, d - 1], g_s.at[way, d - 1], g_r.at[way, d - 1], toward[way]
        )

    def rs_flow(d, way, chunk, slot, other, first):
        lines = part(chunk)
        if not first:
            rs_copy(d + 1, way, chunk, slot).wait_recv()
        for r in range(0, half, 16):
            some = pl.ds(chunk * half + r, 16)
            total = rows[slot, some].astype(F32) + rpart[other, some].astype(F32)
            if not first:
                total = total + land[way, d, some].astype(F32)
            rows[slot, some] = total.astype(BF16)
        rs_copy(d, way, chunk, slot).start()
        if chunk == 0:
            if not first:
                g_copy(d + 1, way, slot).wait_recv()
            gsum = grows[slot].astype(F32) + gpart[other].astype(F32)
            if not first:
                gsum = gsum + gland[way, d].astype(F32)
            grows[slot] = gsum.astype(BF16)
            g_copy(d, way, slot).start()

    def near(d, way):
        return own_slot(d, 1 - way), 2 * d - way

    def unit(u, carry):
        i = u // 2
        even = lax.rem(u, 2) == 0

        @pl.when(u == 1)
        def _():
            poll(0, 1)

        @pl.when(jnp.logical_and(even, u > 0))
        def _():
            poll(0, i + 1)

        @pl.when(jnp.logical_not(even))
        def _():
            poll(1, i + 1)

        @pl.when(u == 0)
        def _():
            for k, ref in ((0, x_all), (1, dy_all), (2, p_all)):
                send(ref.at[0], ref.at[1], pc_s.at[k, 0, 0], pc_r.at[k, 0, 0], partner).wait_recv()

        @pl.when(jnp.logical_and(even, u > 0))
        def _():
            for k, ref in ((0, x_all), (1, dy_all), (2, p_all)):
                for way in range(2):
                    cross(k, ref, i, way).wait_recv()

        @pl.when(u == 2 * steps - 1)
        def _():
            for copy in rows_out(steps - 1):
                copy.wait_recv()
            for way in range(2):
                slot, other = near(steps - 1, way)
                rs_flow(steps - 1, way, 1 - way, slot, other, True)
            for way in range(2):
                cross_half(0, x_all, way).wait_recv()
                cross_half(1, dy_all, way).wait_recv()
            cross_p_last().wait_recv()

        compute(u)

        @pl.when(u == 0)
        def _():
            for copy in rows_first():
                copy.start()

        @pl.when(jnp.logical_and(even, u > 0))
        def _():
            for copy in rows_out(i):
                copy.start()

        @pl.when(u == 2 * steps - 1)
        def _():
            for copy in rows_last():
                copy.start()

        gather_weights(u)
        return carry

    lax.fori_loop(0, 2 * steps, unit, 0)

    for copy in rows_last():
        copy.wait_recv()
    for way in range(2):
        rs_flow(steps, way, way, last_own, 2 * steps - 1, True)

    def w_copies(j):
        to = lax.rem(me_dp + j, ndp)
        return (
            send(stage_g.at[to], land_g.at[j], w_s.at[0, j], w_r.at[0, j], (to, me)),
            send(stage_d.at[to], land_d.at[j], w_s.at[1, j], w_r.at[1, j], (to, me)),
        )

    for n in range(ndp):
        stage_g[n] = acc_gu[n * cut_g : (n + 1) * cut_g, :].astype(BF16)
    for n in range(ndp):
        stage_d[n] = acc_d[n * cut_d : (n + 1) * cut_d, :].astype(BF16)

    @pl.when(n_ahead < len(peers))
    def _():
        pl.semaphore_wait(ready_sem, len(peers) - n_ahead)

    for j in range(1, ndp):
        for copy in w_copies(j):
            copy.start()

    def ring(t, carry):
        d = steps - 1 - t
        for way in range(2):
            slot, other = near(d, way)
            rs_flow(d, way, way, slot, other, False)

        @pl.when(d >= 2)
        def _():
            rp_wait = rows_out(d - 1)
            for copy in rp_wait:
                copy.wait_recv()
            for way in range(2):
                slot, other = near(d - 1, way)
                rs_flow(d - 1, way, 1 - way, slot, other, False)

        return carry

    lax.fori_loop(0, steps - 1, ring, 0)

    for j in range(1, ndp):
        for copy in w_copies(j):
            copy.wait_recv()
    sum_g = stage_g[me_dp].astype(F32)
    sum_d = stage_d[me_dp].astype(F32)
    for j in range(1, ndp):
        sum_g = sum_g + land_g[j].astype(F32)
        sum_d = sum_d + land_d[j].astype(F32)
    og_ref[0] = sum_g[:, :ff].astype(BF16)
    ou_ref[0] = sum_g[:, ff:].astype(BF16)
    od_ref[0] = sum_d.astype(BF16)

    for copy in rows_first():
        copy.wait_recv()
    for way in range(2):
        rs_copy(1, way, 1 - way, 0).wait_recv()
    for way in range(2):
        rs_copy(1, way, way, 0).wait_recv()
        g_copy(1, way, 0).wait_recv()
    for r in range(0, tok, 16):
        some = pl.ds(r, 16)
        total = rows[0, some].astype(F32) + rpart[0, some].astype(F32)
        total = total + land[0, 0, some].astype(F32) + land[1, 0, some].astype(F32)
        gt_ref[some, :] = total.astype(BF16)
    gsum = grows[0].astype(F32) + gpart[0].astype(F32) + gland[0, 0].astype(F32) + gland[1, 0].astype(F32)
    picked = []
    for k in range(topk):
        picked.append(jnp.sum(jnp.where(line == ids_ref[k : k + 1, :], gsum, 0.0), axis=0, keepdims=True))
    gp_ref[...] = jnp.concatenate(picked, axis=0).astype(BF16)

    for k, src in ((0, x_ref), (1, dy_ref), (2, p_all.at[0])):
        ref = (x_all, dy_all, p_all)[k]
        for way in range(2):
            send(src, ref.at[own_slot(1, way)], ag_s.at[k, 1, way], ag_r.at[k, 1, way], toward[way]).wait_send()
        send(src, ref.at[1], pc_s.at[k, 0, 0], pc_r.at[k, 0, 0], partner).wait_send()

    def drain(s, carry):
        for k, ref in ((0, x_all), (1, dy_all), (2, p_all)):
            for way in range(2):
                cross(k, ref, s, way).wait_send()

                @pl.when(s < steps - 1)
                def _():
                    forward(k, ref, s, way).wait_send()

        for copy in rows_out(s):
            copy.wait_send()
        for way in range(2):
            slot, _ = near(s, way)
            for chunk in range(2):
                rs_copy(s, way, chunk, slot).wait_send()
            g_copy(s, way, slot).wait_send()
        return carry

    lax.fori_loop(1, steps, drain, 0)
    for k, ref in ((0, x_all), (1, dy_all)):
        for way in range(2):
            forward_half(k, ref, way).wait_send()
            cross_half(k, ref, way).wait_send()
    forward_p_last().wait_send()
    cross_p_last().wait_send()
    for copy in rows_first() + rows_last():
        copy.wait_send()
    for way in range(2):
        rs_copy(steps, way, way, last_own).wait_send()
    g_copy(steps, 0, last_own).wait_send()
    for j in range(1, ndp):
        for copy in w_copies(j):
            copy.wait_send()


def hand_on(*refs):
    for src, dst in zip(refs[:5], refs[5:]):
        dst[...] = src[...]


def on_device(tokens, cotangent, expert_ids, gate_probs, w_gate, w_up, w_down):
    ndp, nex = lax.axis_size("dp"), lax.axis_size("expert")
    steps = nex // 4
    tok, width = tokens.shape
    ff = w_gate.shape[2]
    topk = expert_ids.shape[1]
    cut_g, cut_d = width // ndp, ff // ndp
    blocks = 4 * steps
    vmem = pl.BlockSpec(memory_space=pltpu.VMEM)
    hbm = pl.BlockSpec(memory_space=pl.ANY)
    dma = pltpu.SemaphoreType.DMA
    outs = pl.pallas_call(
        kernel,
        out_shape=(
            jax.ShapeDtypeStruct((tok, width), BF16),
            jax.ShapeDtypeStruct((topk, tok), BF16),
            jax.ShapeDtypeStruct((1, cut_g, ff), BF16),
            jax.ShapeDtypeStruct((1, cut_g, ff), BF16),
            jax.ShapeDtypeStruct((1, cut_d, width), BF16),
        ),
        in_specs=[vmem, vmem, hbm, hbm, hbm, hbm, hbm],
        out_specs=[vmem] * 5,
        scratch_shapes=[
            pltpu.VMEM((blocks, tok, width), BF16),
            pltpu.VMEM((blocks, tok, width), BF16),
            pltpu.VMEM((blocks, nex, tok), BF16),
            pltpu.VMEM((blocks, tok, width), BF16),
            pltpu.VMEM((blocks, nex, tok), BF16),
            pltpu.VMEM((blocks // 2, tok, width), BF16),
            pltpu.VMEM((blocks // 2, nex, tok), BF16),
            pltpu.VMEM((2, steps, tok, width), BF16),
            pltpu.VMEM((2, steps, nex, tok), BF16),
            pltpu.VMEM((width, 2 * ff), BF16),
            pltpu.VMEM((ff, width), BF16),
            pltpu.VMEM((width, 2 * ff), F32),
            pltpu.VMEM((ff, width), F32),
            pltpu.VMEM((2 * tok, 2 * ff), F32),
            pltpu.VMEM((2 * tok, ff), F32),
            pltpu.VMEM((2 * tok, 2 * ff), BF16),
            pltpu.VMEM((2 * tok, ff), BF16),
            pltpu.VMEM((ndp, cut_g, 2 * ff), BF16),
            pltpu.VMEM((ndp, cut_d, width), BF16),
            pltpu.VMEM((ndp, cut_g, 2 * ff), BF16),
            pltpu.VMEM((ndp, cut_d, width), BF16),
            dma((3, steps + 1, 2)),
            dma((3, steps + 1, 2)),
            dma((3, steps + 1, 2)),
            dma((3, steps + 1, 2)),
            dma((2, steps + 1)),
            dma((2, steps + 1)),
            dma((2, 2, steps)),
            dma((2, 2, steps)),
            dma((2, steps)),
            dma((2, steps)),
            dma((2, ndp)),
            dma((2, ndp)),
            dma((5,)),
            pltpu.SemaphoreType.REGULAR,
        ],
        compiler_params=pltpu.CompilerParams(
            collective_id=0, has_side_effects=True, vmem_limit_bytes=63 * 1024 * 1024
        ),
        name="moe_backward",
    )(expert_ids.T, gate_probs.T, tokens, cotangent, w_gate, w_up, w_down)
    outs = pl.pallas_call(
        hand_on,
        out_shape=[jax.ShapeDtypeStruct(v.shape, v.dtype) for v in outs],
        in_specs=[vmem] * 5,
        out_specs=[vmem] * 5,
        name="hand_on",
    )(*outs)
    return outs[0], outs[1].T, outs[2], outs[3], outs[4]


def solution(mesh):
    return jax.shard_map(
        on_device,
        mesh=mesh,
        in_specs=(
            P(("dp", "expert"), None),
            P(("dp", "expert"), None),
            P(("dp", "expert"), None),
            P(("dp", "expert"), None),
            P("expert", None, None),
            P("expert", None, None),
            P("expert", None, None),
        ),
        out_specs=(
            P(("dp", "expert"), None),
            P(("dp", "expert"), None),
            P("expert", "dp", None),
            P("expert", "dp", None),
            P("expert", "dp", None),
        ),
        check_vma=False,
    )
```
